32 devices in a mesh: ia: 16 (over z, x, core), jb: 2 (over y).
Axes of the slice: x: 2, y: 2, z: 4, core: 2. Of those that a mesh axis runs over, the one named last changes fastest.
Arguments:
- density: bfloat16 [8000, 100000], P('ia', 'jb'), may hold values from -6 to 6
- chol_vectors: bfloat16 [100000, 32], P('jb', 'ia'), may hold values from -0.01953125 to 0.01953125
- virt_coef: bfloat16 [1000, 1100], P('jb'), may hold values from -0.1875 to 0.1875
Outputs:
- half_back: float32 [8, 32, 1100], P(None, ('ia', 'jb'))
The draws below stay inside these ranges and needn't reach their ends.
All inputs are finite; a program needn't handle non-finite values.
Results may differ from the reference program's by a relative error of at most 0.0003.
Values may be sent and summed in bfloat16 or wider, within the bound.
A program may use at most 128 MiB of HBM per device.

```python
import jax
import jax.numpy as jnp
from jax import lax

NOCC = 100
NV = 1000
NAO = 1100
OSLAB = 8
NCHOL = 32


def level_of(rng, extent, cuts, smallest, high):
    level, own = 1.0, jax.random.fold_in(rng, 6)
    for dim, shards_of in cuts:
        heights = jnp.exp(jax.random.uniform(jax.random.fold_in(own, dim), (shards_of,), jnp.float32, smallest / len(cuts), high / len(cuts)))
        level = level * jnp.repeat(heights, extent[dim] // shards_of).reshape([-1 if axis == dim else 1 for axis in range(len(extent))])
    return level


def noise(stream_key, shape, scale, most, cuts=(), dtype=jnp.bfloat16):
    entries = jax.random.normal(stream_key, shape, jnp.float32) * scale
    if len(cuts) > 0:
        entries = level_of(stream_key, shape, cuts, -0.22, 0.18) * entries
    return jnp.clip(entries, min=-most, max=most).astype(dtype)


def setup_inputs(seed: int = 0) -> dict:
    keys = jax.random.split(jax.random.key(seed), 4)
    return {
        "density": noise(keys[0], (OSLAB * NV, NOCC * NV), 1.0, 6.0, ((0, 16), (1, 2))),
        "chol_vectors": noise(keys[1], (NOCC * NV, NCHOL), (NOCC * NV) ** -0.5, 0.01953125, ((0, 2), (1, 16))),
        "virt_coef": noise(keys[2], (NV, NAO), NV ** -0.5, 0.1875, ((0, 2),)),
    }


def reference(density, chol_vectors, virt_coef):
    gamma_full = jnp.dot(density, chol_vectors, preferred_element_type=jnp.float32)
    gamma_full = gamma_full.reshape(OSLAB, NV, NCHOL)
    return jnp.einsum("iap,an->ipn", gamma_full, virt_coef.astype(jnp.float32), precision=lax.Precision.HIGHEST)
```

```python
import functools

import jax
import jax.numpy as jnp
from jax import lax
from jax.experimental import pallas as pl
from jax.experimental.pallas import tpu as pltpu
from jax.sharding import PartitionSpec as P

MESH = pl.DeviceIdType.MESH
LANES = 128
VMEM_BYTES = 67043328
PARTS = 13
BEFORE = 2
Z_LAG = 2
X_LAG = 5
K_LAG = 6
NT = (((1,), (1,)), ((), ()))


def from_root(value, axis, source):
    kept = jnp.where(lax.axis_index(axis) == source, value, 0).astype(value.dtype)
    return lax.psum(kept, axis)


def by_collectives(density, chol_vectors, virt_coef):
    row_count = density.shape[0]
    groups = lax.axis_size("jb")
    slab_devices = lax.axis_size("ia")
    all_vectors = lax.all_gather(chol_vectors, "ia", axis=1, tiled=True)
    gamma_part = jnp.dot(density, all_vectors, preferred_element_type=jnp.float32)
    owner_row = lax.axis_index("ia") % groups
    coef_block = from_root(virt_coef, "jb", owner_row).astype(jnp.float32)
    chol_count = gamma_part.shape[1]
    group_width = chol_count // slab_devices
    reduced = lax.psum_scatter(
        gamma_part.reshape(row_count, slab_devices, group_width),
        "jb",
        scatter_dimension=2,
        tiled=True,
    )
    summed = jnp.einsum("arq,an->rqn", reduced, coef_block, precision=lax.Precision.HIGHEST)
    regrouped = lax.all_to_all(summed, "ia", split_axis=0, concat_axis=0, tiled=True)
    occ_slab = slab_devices // groups
    return jnp.sum(
        regrouped.reshape(occ_slab, groups, regrouped.shape[1], regrouped.shape[2]), axis=1
    )


def chunk_of(columns):
    return columns // (PARTS * LANES) * LANES


def kernel(
    slab, groups, d_hbm, v_hbm, c_hbm, o_ref,
    dbuf, vbuf, cbuf, acc, gsend, grecv,
    dsem, lsem, zs, zr, ws, wr, xs, xr, fs, fr, ks, kr, cs, cr, gs, gr, other,
):
    width, columns = v_hbm.shape
    unit = chunk_of(columns)
    last = PARTS - 1
    last_size = columns - last * unit
    total = slab * groups
    occ = slab // groups
    half_slots = slab // 2
    r, g = lax.axis_index("ia"), lax.axis_index("jb")
    z, x, k = r // 4, (r // 2) % 2, r % 2
    inner = ((z + 1) // 2) % 2
    linear = r * groups + g

    def ring(zz, xx, kk):
        return ((zz * 2 + xx) * 2 + kk, g)

    flip = {1: z + 1 - 2 * (z % 2), 2: (z + 2) % 4, 3: 3 - z}
    x_mate = ring(z, 1 - x, k)
    k_mate = ring(z, x, 1 - k)
    y_mate = (r, 1 - g)

    def device(lin):
        return (lin // groups, lin % groups)

    def slot_of(rr):
        zz, xx, kk = rr // 4, (rr // 2) % 2, rr % 2
        other_x, other_k = (xx + x) % 2, (kk + k) % 2
        near = jnp.where((zz // 2) == (z // 2), jnp.where(zz == z, 0, 3 - 2 * inner), 0)
        far = jnp.where((zz // 2) == (z // 2), 0, jnp.where(zz + z == 3, 1 + 2 * inner, 2))
        return (other_k * 2 + other_x) * 4 + near + far

    def cols(j):
        if isinstance(j, int) and j == last:
            return pl.ds(last * unit, last_size)
        return pl.ds(pl.multiple_of(j * unit, LANES), unit)

    def each(j, f):
        pl.when(j < last)(lambda: f(j))
        pl.when(j == last)(lambda: f(last))

    whole = pl.ds(0, columns)
    relayed = pl.ds(0, columns - last_size)

    def rows(start, size):
        if isinstance(start, int):
            return pl.ds(start * width, size * width)
        return pl.ds(pl.multiple_of(start * width, width), size * width)

    def d_copy(j):
        return pltpu.make_async_copy(d_hbm.at[:, cols(j)], dbuf.at[:, cols(j)], dsem.at[j])

    v_local = pltpu.make_async_copy(v_hbm, vbuf.at[rows(0, 1), :], lsem.at[0])
    c_local = pltpu.make_async_copy(c_hbm, cbuf.at[g], lsem.at[1])

    def remote(source, dest, send, recv, target):
        return pltpu.make_async_remote_copy(
            source, dest, send, recv, device_id=target, device_id_type=MESH
        )

    def z_part(part, step, recv):
        slot = 2 if step == 2 else 1 + 2 * inner
        return remote(
            v_hbm.at[:, part], vbuf.at[rows(slot, 1), part],
            zs.at[step - 1], recv, ring(flip[step], x, k),
        )

    def z_copy(j, step):
        return z_part(cols(j), step, zr.at[j, step - 1])

    def z_pass(j):
        return remote(
            vbuf.at[rows(3, 1), cols(j)], vbuf.at[rows(2, 1), cols(j)],
            zs.at[1], zr.at[j, 1], ring(flip[1], x, k),
        )

    def w_part(part, recv):
        return remote(v_hbm.at[:, part], vbuf.at[rows(4, 1), part], ws, recv, x_mate)

    def w_copy(j):
        return w_part(cols(j), wr.at[j])

    def x_part(part, recv):
        return remote(vbuf.at[rows(1, 3), part], vbuf.at[rows(5, 3), part], xs, recv, x_mate)

    def x_copy(j):
        return x_part(cols(j), xr.at[j])

    def f_copy(step):
        slot = 6 if step == 2 else 5 + 2 * inner
        return remote(
            vbuf.at[rows(4, 1), cols(last)], vbuf.at[rows(slot, 1), cols(last)],
            fs.at[step - 1], fr.at[step - 1], ring(flip[step], x, k),
        )

    def k_part(part, recv):
        return remote(
            vbuf.at[rows(0, half_slots), part], vbuf.at[rows(half_slots, half_slots), part],
            ks, recv, k_mate,
        )

    def k_copy(j):
        return k_part(cols(j), kr.at[j])

    orbitals = c_hbm.shape[0]
    cut = orbitals // 32 * 16
    halves = (pl.ds(0, cut), pl.ds(cut, orbitals - cut))

    def c_over(half):
        return remote(
            c_hbm.at[halves[half], :], cbuf.at[g, halves[half], :], cs.at[0], cr.at[0], y_mate
        )

    def c_across(half):
        part = cbuf.at[1 - g, halves[half], :]
        return remote(part, part, cs.at[1], cr.at[1], k_mate)

    def by_core(f):
        for half in range(2):
            pl.when(k == half)(functools.partial(f, half))

    def looped(f, start, stop):
        def body(j, carry):
            f(j)
            return carry

        lax.fori_loop(start, stop, body, 0)

    v_local.start()
    looped(lambda j: d_copy(j).start(), 0, last)
    d_copy(last).start()
    c_local.start()

    barrier = pltpu.get_barrier_semaphore()
    mates = [ring(flip[step], x, k) for step in (1, 2, 3)] + [x_mate, k_mate, y_mate]
    for mate in mates:
        pl.semaphore_signal(barrier, inc=1, device_id=mate, device_id_type=MESH)
    pl.semaphore_wait(barrier, len(mates))

    def own_send(j):
        z_copy(j, 3).start()
        pl.when(inner == 0)(lambda: z_copy(j, 2).start())
        pl.when((inner == 0) | (j < BEFORE))(lambda: z_copy(j, 1).start())
        w_copy(j).start()

    w_copy(last).start()
    looped(own_send, 0, last)
    for step in (3, 2):
        z_copy(last, step).start()
    pl.when(inner == 0)(lambda: z_copy(last, 1).start())
    by_core(lambda half: c_over(half).start())
    acc[...] = jnp.zeros_like(acc)
    v_local.wait()
    w_copy(last).wait_recv()
    for step in (3, 2, 1):
        f_copy(step).start()

    def z_relay(j):
        z_copy(j, 3).wait_recv()
        z_pass(j).start()
        pl.when(j + BEFORE <= last)(
            lambda: each(j + BEFORE, lambda i: z_copy(i, 1).start())
        )

    def x_relay(j):
        z_copy(j, 1).wait_recv()
        z_copy(j, 2).wait_recv()
        pl.when(inner == 0)(lambda: z_copy(j, 3).wait_recv())
        x_copy(j).start()

    def k_relay(j):
        if isinstance(j, int):
            for step in (1, 2, 3):
                z_copy(j, step).wait_recv()
                f_copy(step).wait_recv()
        else:
            w_copy(j).wait_recv()
            x_copy(j).wait_recv()
        k_copy(j).start()

    def landed(j):
        k_copy(j).wait_recv()
        d_copy(j).wait()

    def add_product(part):
        acc[...] += lax.dot_general(
            dbuf[:, part], vbuf[:, part], NT, preferred_element_type=jnp.float32
        )

    def multiply(j):
        each(j, landed)
        add_product(pl.ds(pl.multiple_of(j * unit, LANES), unit))
        if last_size > unit:
            spare = pl.ds(PARTS * unit, last_size - unit)
            pl.when(j == last)(lambda: add_product(spare))

        @pl.when(j == 0)
        def _():
            pl.semaphore_signal(other, inc=1, device_id=y_mate, device_id_type=MESH)

    def c_pass(half):
        c_over(half).wait_recv()
        c_across(half).start()

    def step_of(t):
        pl.when((inner == 1) & (t < last))(lambda: z_relay(t))
        middle = t - Z_LAG
        pl.when((middle >= 0) & (middle < last))(lambda: x_relay(middle))
        before = t - X_LAG
        pl.when(before >= 0)(lambda: each(before, k_relay))
        done = t - K_LAG
        pl.when(done >= 0)(lambda: multiply(done))
        pl.when(t == PARTS)(lambda: by_core(c_pass))

    looped(step_of, 0, PARTS + K_LAG)

    gsend[:, 0, :] = acc[...].T
    pl.semaphore_wait(other, 1)

    own_place = grecv.at[g, r % groups, r // groups]

    def g_copy(step):
        target = (linear + step) % total
        tr, tg = device(target)
        return remote(gsend.at[slot_of(tr) * width + tg], own_place, gs, gr, (tr, tg))

    looped(lambda step: g_copy(step).start(), 1, total)
    pltpu.make_async_copy(gsend.at[g], own_place, gr).start()

    for step in (1, 2, 3):
        z_part(whole, step, zr.at[0, step - 1]).wait_send()
        f_copy(step).wait_send()
    w_part(whole, wr.at[0]).wait_send()
    x_part(relayed, xr.at[0]).wait_send()
    k_part(whole, kr.at[0]).wait_send()
    c_local.wait()

    def c_done(half):
        c_over(half).wait_send()
        c_across(half).wait_send()
        c_across(1 - half).wait_recv()

    by_core(c_done)
    pltpu.make_async_copy(grecv, grecv, gr).wait()

    total_out = None
    for half in range(groups):
        gam = sum(grecv[src, half, :, 0, :] for src in range(1, groups)) + grecv[0, half, :, 0, :]
        high = gam.astype(jnp.bfloat16).astype(jnp.float32)
        left = gam - high
        mid = left.astype(jnp.bfloat16).astype(jnp.float32)
        low = left - mid
        stacked = jnp.concatenate([high, mid, low], axis=0).astype(jnp.bfloat16)
        part = lax.dot_general(stacked, cbuf[half], NT, preferred_element_type=jnp.float32)
        total_out = part if total_out is None else total_out + part
    o_ref[...] = total_out[2 * occ:] + total_out[occ:2 * occ] + total_out[:occ]
    outgoing = gsend.at[pl.ds(0, total - 1)]
    pltpu.make_async_copy(outgoing, outgoing, gs).wait()


def fused(slab, groups, density, chol_vectors, virt_coef):
    rows, columns = density.shape
    width = chol_vectors.shape[1]
    coef_rows, orbitals = virt_coef.shape
    total, occ = slab * groups, slab // groups
    dma = pltpu.SemaphoreType.DMA
    out = pl.pallas_call(
        functools.partial(kernel, slab, groups),
        out_shape=jax.ShapeDtypeStruct((occ, orbitals), jnp.float32),
        in_specs=[pl.BlockSpec(memory_space=pl.ANY)] * 3,
        out_specs=pl.BlockSpec(memory_space=pltpu.VMEM),
        scratch_shapes=[
            pltpu.VMEM((rows, columns), density.dtype),
            pltpu.VMEM((slab * width, columns), chol_vectors.dtype),
            pltpu.VMEM((groups, orbitals, coef_rows), virt_coef.dtype),
            pltpu.VMEM((rows, slab * width), jnp.float32),
            pltpu.VMEM((slab * width, 1, rows), jnp.float32),
            pltpu.VMEM((groups, groups, occ, 1, rows), jnp.float32),
            dma((PARTS,)), dma((2,)),
            dma((3,)), dma((PARTS, 3)), dma, dma((PARTS,)),
            dma, dma((PARTS,)), dma((3,)), dma((3,)), dma, dma((PARTS,)),
            dma((2,)), dma((2,)), dma, dma, pltpu.SemaphoreType.REGULAR,
        ],
        compiler_params=pltpu.CompilerParams(
            collective_id=0, has_side_effects=True, vmem_limit_bytes=VMEM_BYTES
        ),
    )(density, chol_vectors.T, virt_coef.T)
    return out.reshape(occ, 1, orbitals)


def on_device(slab, groups, density, chol_vectors, virt_coef):
    rows, columns = density.shape
    width = chol_vectors.shape[1]
    padded = (columns + LANES) * (rows + 16 + slab * width) * 2
    fits = padded + 8 * virt_coef.size < VMEM_BYTES - (6 << 20)
    paired = groups == 2 and width == groups and slab == 16
    if fits and paired and rows == virt_coef.shape[0] and chunk_of(columns) > 0:
        return fused(slab, groups, density, chol_vectors, virt_coef)
    return by_collectives(density, chol_vectors, virt_coef)


def solution(mesh):
    in_specs = (P("ia", "jb"), P("jb", "ia"), P("jb", None))
    out_specs = P(None, ("ia", "jb"), None)
    body = functools.partial(on_device, mesh.shape["ia"], mesh.shape["jb"])
    return jax.shard_map(body, mesh=mesh, in_specs=in_specs, out_specs=out_specs, check_vma=False)
```

```python
import functools

import jax
import jax.numpy as jnp
from jax import lax
from jax.experimental import pallas as pl
from jax.experimental.pallas import tpu as pltpu
from jax.sharding import PartitionSpec as P

MESH = pl.DeviceIdType.MESH
LANES = 128
VMEM_BYTES = 67043328
PARTS = 13
BEFORE = 2
PACED = 3
Z_LAG = 1
X_LAG = 4
K_LAG = 5
NT = (((1,), (1,)), ((), ()))


def from_root(value, axis, source):
    kept = jnp.where(lax.axis_index(axis) == source, value, 0).astype(value.dtype)
    return lax.psum(kept, axis)


def by_collectives(density, chol_vectors, virt_coef):
    row_count = density.shape[0]
    groups = lax.axis_size("jb")
    slab_devices = lax.axis_size("ia")
    all_vectors = lax.all_gather(chol_vectors, "ia", axis=1, tiled=True)
    gamma_part = jnp.dot(density, all_vectors, preferred_element_type=jnp.float32)
    owner_row = lax.axis_index("ia") % groups
    coef_block = from_root(virt_coef, "jb", owner_row).astype(jnp.float32)
    chol_count = gamma_part.shape[1]
    group_width = chol_count // slab_devices
    reduced = lax.psum_scatter(
        gamma_part.reshape(row_count, slab_devices, group_width),
        "jb",
        scatter_dimension=2,
        tiled=True,
    )
    summed = jnp.einsum("arq,an->rqn", reduced, coef_block, precision=lax.Precision.HIGHEST)
    regrouped = lax.all_to_all(summed, "ia", split_axis=0, concat_axis=0, tiled=True)
    occ_slab = slab_devices // groups
    return jnp.sum(
        regrouped.reshape(occ_slab, groups, regrouped.shape[1], regrouped.shape[2]), axis=1
    )


def chunk_of(columns):
    return columns // (PARTS * LANES) * LANES


def kernel(
    slab, groups, d_hbm, v_hbm, c_hbm, o_ref,
    dbuf, vbuf, cbuf, acc, bcc, gsend, grecv,
    dsem, lsem, zs, zr, ws, wr, xs, xr, ks, kr, cs, cr, gs, gr, other,
):
    width, columns = v_hbm.shape
    unit = chunk_of(columns)
    last = PARTS - 1
    last_size = columns - last * unit
    total = slab * groups
    occ = slab // groups
    half_slots = slab // 2
    r, g = lax.axis_index("ia"), lax.axis_index("jb")
    z, x, k = r // 4, (r // 2) % 2, r % 2
    inner = ((z + 1) // 2) % 2
    linear = r * groups + g

    def ring(zz, xx, kk):
        return ((zz * 2 + xx) * 2 + kk, g)

    flip = {1: z + 1 - 2 * (z % 2), 2: (z + 2) % 4, 3: 3 - z}
    x_mate = ring(z, 1 - x, k)
    k_mate = ring(z, x, 1 - k)
    y_mate = (r, 1 - g)

    def device(lin):
        return (lin // groups, lin % groups)

    def slot_of(rr):
        zz, xx, kk = rr // 4, (rr // 2) % 2, rr % 2
        other_x, other_k = (xx + x) % 2, (kk + k) % 2
        near = jnp.where((zz // 2) == (z // 2), jnp.where(zz == z, 0, 3 - 2 * inner), 0)
        far = jnp.where((zz // 2) == (z // 2), 0, jnp.where(zz + z == 3, 1 + 2 * inner, 2))
        return (other_k * 2 + other_x) * 4 + near + far

    def cols(j):
        if isinstance(j, int) and j == last:
            return pl.ds(last * unit, last_size)
        return pl.ds(pl.multiple_of(j * unit, LANES), unit)

    def each(j, f):
        pl.when(j < last)(lambda: f(j))
        pl.when(j == last)(lambda: f(last))

    whole = pl.ds(0, columns)

    def rows(start, size):
        if isinstance(start, int):
            return pl.ds(start * width, size * width)
        return pl.ds(pl.multiple_of(start * width, width), size * width)

    def d_copy(j):
        return pltpu.make_async_copy(d_hbm.at[:, cols(j)], dbuf.at[:, cols(j)], dsem.at[j])

    v_local = pltpu.make_async_copy(v_hbm, vbuf.at[rows(0, 1), :], lsem.at[0])
    c_local = pltpu.make_async_copy(c_hbm, cbuf.at[g], lsem.at[1])

    def remote(source, dest, send, recv, target):
        return pltpu.make_async_remote_copy(
            source, dest, send, recv, device_id=target, device_id_type=MESH
        )

    def z_part(part, step, recv):
        slot = 2 if step == 2 else 1 + 2 * inner
        return remote(
            v_hbm.at[:, part], vbuf.at[rows(slot, 1), part],
            zs.at[step - 1], recv, ring(flip[step], x, k),
        )

    def z_copy(j, step):
        return z_part(cols(j), step, zr.at[j, step - 1])

    def z_pass(j):
        return remote(
            vbuf.at[rows(3, 1), cols(j)], vbuf.at[rows(2, 1), cols(j)],
            zs.at[1], zr.at[j, 1], ring(flip[1], x, k),
        )

    def w_part(part, recv):
        return remote(v_hbm.at[:, part], vbuf.at[rows(4, 1), part], ws, recv, x_mate)

    def w_copy(j):
        return w_part(cols(j), wr.at[j])

    def x_part(part, recv):
        return remote(vbuf.at[rows(1, 3), part], vbuf.at[rows(5, 3), part], xs, recv, x_mate)

    def x_copy(j):
        return x_part(cols(j), xr.at[j])

    def k_part(part, recv):
        return remote(
            vbuf.at[rows(0, half_slots), part], vbuf.at[rows(half_slots, half_slots), part],
            ks, recv, k_mate,
        )

    def k_copy(j):
        return k_part(cols(j), kr.at[j])

    orbitals = c_hbm.shape[0]
    cut = orbitals // 32 * 16
    halves = (pl.ds(0, cut), pl.ds(cut, orbitals - cut))

    def c_over(half):
        return remote(
            c_hbm.at[halves[half], :], cbuf.at[g, halves[half], :], cs.at[0], cr.at[0], y_mate
        )

    def c_across(half):
        part = cbuf.at[1 - g, halves[half], :]
        return remote(part, part, cs.at[1], cr.at[1], k_mate)

    def by_core(f):
        for half in range(2):
            pl.when(k == half)(functools.partial(f, half))

    def looped(f, start, stop):
        def body(j, carry):
            f(j)
            return carry

        lax.fori_loop(start, stop, body, 0)

    v_local.start()
    looped(lambda j: d_copy(j).start(), 0, last)
    d_copy(last).start()
    c_local.start()

    barrier = pltpu.get_barrier_semaphore()
    mates = [ring(flip[step], x, k) for step in (1, 2, 3)] + [x_mate, k_mate, y_mate]
    for mate in mates:
        pl.semaphore_signal(barrier, inc=1, device_id=mate, device_id_type=MESH)
    pl.semaphore_wait(barrier, len(mates))

    def own_send(i):
        def send(j):
            z_copy(j, 3).start()
            pl.when(inner == 0)(lambda: z_copy(j, 2).start())
            pl.when((inner == 0) | (i < BEFORE))(lambda: z_copy(j, 1).start())
            w_copy(j).start()

        each(i, send)

    looped(own_send, 0, PACED)
    pl.when(k == 0)(lambda: looped(own_send, PACED, PARTS))
    by_core(lambda half: c_over(half).start())
    acc[...] = jnp.zeros_like(acc)
    bcc[...] = jnp.zeros_like(bcc)
    v_local.wait()

    def z_relay(j):
        z_copy(j, 3).wait_recv()
        z_pass(j).start()
        pl.when(j + BEFORE <= last)(
            lambda: each(j + BEFORE, lambda i: z_copy(i, 1).start())
        )

    def x_relay(j):
        z_copy(j, 1).wait_recv()
        z_copy(j, 2).wait_recv()
        pl.when(inner == 0)(lambda: z_copy(j, 3).wait_recv())
        x_copy(j).start()

    def k_relay(j):
        w_copy(j).wait_recv()
        x_copy(j).wait_recv()
        k_copy(j).start()

    def landed(j):
        k_copy(j).wait_recv()
        d_copy(j).wait()

    top = acc.shape[0]

    def add_product(part):
        upper = lax.dot_general(
            dbuf[0:top, part], vbuf[:, part], NT, preferred_element_type=jnp.float32
        )
        lower = lax.dot_general(
            vbuf[:, part], dbuf[top:, part], NT, preferred_element_type=jnp.float32
        )
        acc[...] += upper
        bcc[...] += lower

    def multiply(j):
        each(j, landed)
        add_product(pl.ds(pl.multiple_of(j * unit, LANES), unit))
        if columns > PARTS * unit:
            spare = pl.ds(PARTS * unit, columns - PARTS * unit)
            pl.when(j == PARTS - 1)(lambda: add_product(spare))

        @pl.when(j == 0)
        def _():
            pl.semaphore_signal(other, inc=1, device_id=y_mate, device_id_type=MESH)

    def c_pass(half):
        c_over(half).wait_recv()
        c_across(half).start()

    def step_of(t):
        pl.when(inner == 1)(lambda: each(t, z_relay))
        pl.when((k == 1) & (t + PACED < PARTS))(lambda: own_send(t + PACED))
        middle = t - Z_LAG
        pl.when(middle >= 0)(lambda: each(middle, x_relay))
        before = t - X_LAG
        pl.when(before >= 0)(lambda: each(before, k_relay))
        done = t - K_LAG
        pl.when(done >= 0)(lambda: multiply(done))
        pl.when(t == PARTS)(lambda: by_core(c_pass))

    looped(step_of, 0, PARTS + K_LAG)

    gsend[:, 0, 0:top] = acc[...].T
    gsend[:, 0, top:] = bcc[...]
    pl.semaphore_wait(other, 1)

    own_place = grecv.at[g, r % groups, r // groups]

    def g_copy(step):
        target = (linear + step) % total
        tr, tg = device(target)
        return remote(gsend.at[slot_of(tr) * width + tg], own_place, gs, gr, (tr, tg))

    looped(lambda step: g_copy(step).start(), 1, total)
    pltpu.make_async_copy(gsend.at[g], own_place, gr).start()

    for step in (1, 2, 3):
        z_part(whole, step, zr.at[0, step - 1]).wait_send()
    w_part(whole, wr.at[0]).wait_send()
    x_part(whole, xr.at[0]).wait_send()
    k_part(whole, kr.at[0]).wait_send()
    c_local.wait()

    def c_done(half):
        c_over(half).wait_send()
        c_across(half).wait_send()
        c_across(1 - half).wait_recv()

    by_core(c_done)
    pltpu.make_async_copy(grecv, grecv, gr).wait()

    total_out = None
    for half in range(groups):
        gam = sum(grecv[src, half, :, 0, :] for src in range(1, groups)) + grecv[0, half, :, 0, :]
        high = gam.astype(jnp.bfloat16).astype(jnp.float32)
        left = gam - high
        mid = left.astype(jnp.bfloat16).astype(jnp.float32)
        low = left - mid
        stacked = jnp.concatenate([high, mid, low], axis=0).astype(jnp.bfloat16)
        part = lax.dot_general(stacked, cbuf[half], NT, preferred_element_type=jnp.float32)
        total_out = part if total_out is None else total_out + part
    o_ref[...] = total_out[2 * occ:] + total_out[occ:2 * occ] + total_out[:occ]
    outgoing = gsend.at[pl.ds(0, total - 1)]
    pltpu.make_async_copy(outgoing, outgoing, gs).wait()


def fused(slab, groups, density, chol_vectors, virt_coef):
    rows, columns = density.shape
    width = chol_vectors.shape[1]
    coef_rows, orbitals = virt_coef.shape
    total, occ = slab * groups, slab // groups
    top = -(-rows // 256) // 2 * 256
    dma = pltpu.SemaphoreType.DMA
    out = pl.pallas_call(
        functools.partial(kernel, slab, groups),
        out_shape=jax.ShapeDtypeStruct((occ, orbitals), jnp.float32),
        in_specs=[pl.BlockSpec(memory_space=pl.ANY)] * 3,
        out_specs=pl.BlockSpec(memory_space=pltpu.VMEM),
        scratch_shapes=[
            pltpu.VMEM((rows, columns), density.dtype),
            pltpu.VMEM((slab * width, columns), chol_vectors.dtype),
            pltpu.VMEM((groups, orbitals, coef_rows), virt_coef.dtype),
            pltpu.VMEM((top, slab * width), jnp.float32),
            pltpu.VMEM((slab * width, rows - top), jnp.float32),
            pltpu.VMEM((slab * width, 1, rows), jnp.float32),
            pltpu.VMEM((groups, groups, occ, 1, rows), jnp.float32),
            dma((PARTS,)), dma((2,)),
            dma((3,)), dma((PARTS, 3)), dma, dma((PARTS,)),
            dma, dma((PARTS,)), dma, dma((PARTS,)),
            dma((2,)), dma((2,)), dma, dma, pltpu.SemaphoreType.REGULAR,
        ],
        compiler_params=pltpu.CompilerParams(
            collective_id=0, has_side_effects=True, vmem_limit_bytes=VMEM_BYTES
        ),
    )(density, chol_vectors.T, virt_coef.T)
    return out.reshape(occ, 1, orbitals)


def on_device(slab, groups, density, chol_vectors, virt_coef):
    rows, columns = density.shape
    width = chol_vectors.shape[1]
    padded = (columns + LANES) * (rows + 16 + slab * width) * 2
    fits = padded + 8 * virt_coef.size < VMEM_BYTES - (6 << 20)
    paired = groups == 2 and width == groups and slab == 16
    if fits and paired and rows == virt_coef.shape[0] and chunk_of(columns) > 0 and rows > 256:
        return fused(slab, groups, density, chol_vectors, virt_coef)
    return by_collectives(density, chol_vectors, virt_coef)


def solution(mesh):
    in_specs = (P("ia", "jb"), P("jb", "ia"), P("jb", None))
    out_specs = P(None, ("ia", "jb"), None)
    body = functools.partial(on_device, mesh.shape["ia"], mesh.shape["jb"])
    return jax.shard_map(body, mesh=mesh, in_specs=in_specs, out_specs=out_specs, check_vma=False)
```

```python
import functools

import jax
import jax.numpy as jnp
from jax import lax
from jax.experimental import pallas as pl
from jax.experimental.pallas import tpu as pltpu
from jax.sharding import PartitionSpec as P

MESH = pl.DeviceIdType.MESH
LANES = 128
VMEM_BYTES = 67043328
PARTS = 13
BEFORE = 2
PACED = 3
Z_LAG = 1
X_LAG = 4
K_LAG = 5
NT = (((1,), (1,)), ((), ()))


def from_root(value, axis, source):
    kept = jnp.where(lax.axis_index(axis) == source, value, 0).astype(value.dtype)
    return lax.psum(kept, axis)


def by_collectives(density, chol_vectors, virt_coef):
    row_count = density.shape[0]
    groups = lax.axis_size("jb")
    slab_devices = lax.axis_size("ia")
    all_vectors = lax.all_gather(chol_vectors, "ia", axis=1, tiled=True)
    gamma_part = jnp.dot(density, all_vectors, preferred_element_type=jnp.float32)
    owner_row = lax.axis_index("ia") % groups
    coef_block = from_root(virt_coef, "jb", owner_row).astype(jnp.float32)
    chol_count = gamma_part.shape[1]
    group_width = chol_count // slab_devices
    reduced = lax.psum_scatter(
        gamma_part.reshape(row_count, slab_devices, group_width),
        "jb",
        scatter_dimension=2,
        tiled=True,
    )
    summed = jnp.einsum("arq,an->rqn", reduced, coef_block, precision=lax.Precision.HIGHEST)
    regrouped = lax.all_to_all(summed, "ia", split_axis=0, concat_axis=0, tiled=True)
    occ_slab = slab_devices // groups
    return jnp.sum(
        regrouped.reshape(occ_slab, groups, regrouped.shape[1], regrouped.shape[2]), axis=1
    )


def chunk_of(columns):
    return columns // (PARTS * LANES) * LANES


def kernel(
    slab, groups, d_hbm, v_hbm, c_hbm, o_ref,
    dbuf, vbuf, cbuf, acc, bcc, gsend, grecv,
    dsem, lsem, zs, zr, ws, wr, xs, xr, ks, kr, cs, cr, gs, gr, other,
):
    width, columns = v_hbm.shape
    unit = chunk_of(columns)
    last = PARTS - 1
    last_size = columns - last * unit
    total = slab * groups
    occ = slab // groups
    half_slots = slab // 2
    r, g = lax.axis_index("ia"), lax.axis_index("jb")
    z, x, k = r // 4, (r // 2) % 2, r % 2
    inner = ((z + 1) // 2) % 2
    linear = r * groups + g

    def ring(zz, xx, kk):
        return ((zz * 2 + xx) * 2 + kk, g)

    flip = {1: z + 1 - 2 * (z % 2), 2: (z + 2) % 4, 3: 3 - z}
    x_mate = ring(z, 1 - x, k)
    k_mate = ring(z, x, 1 - k)
    y_mate = (r, 1 - g)

    def device(lin):
        return (lin // groups, lin % groups)

    def slot_of(rr):
        zz, xx, kk = rr // 4, (rr // 2) % 2, rr % 2
        other_x, other_k = (xx + x) % 2, (kk + k) % 2
        near = jnp.where((zz // 2) == (z // 2), jnp.where(zz == z, 0, 3 - 2 * inner), 0)
        far = jnp.where((zz // 2) == (z // 2), 0, jnp.where(zz + z == 3, 1 + 2 * inner, 2))
        return (other_k * 2 + other_x) * 4 + near + far

    def cols(j):
        if isinstance(j, int) and j == last:
            return pl.ds(last * unit, last_size)
        return pl.ds(pl.multiple_of(j * unit, LANES), unit)

    def each(j, f):
        pl.when(j < last)(lambda: f(j))
        pl.when(j == last)(lambda: f(last))

    whole = pl.ds(0, columns)

    def rows(start, size):
        if isinstance(start, int):
            return pl.ds(start * width, size * width)
        return pl.ds(pl.multiple_of(start * width, width), size * width)

    def d_copy(j):
        return pltpu.make_async_copy(d_hbm.at[:, cols(j)], dbuf.at[:, cols(j)], dsem.at[j])

    v_local = pltpu.make_async_copy(v_hbm, vbuf.at[rows(0, 1), :], lsem.at[0])
    c_local = pltpu.make_async_copy(c_hbm, cbuf.at[g], lsem.at[1])

    def remote(source, dest, send, recv, target):
        return pltpu.make_async_remote_copy(
            source, dest, send, recv, device_id=target, device_id_type=MESH
        )

    def z_part(part, step, recv):
        slot = 2 if step == 2 else 1 + 2 * inner
        return remote(
            v_hbm.at[:, part], vbuf.at[rows(slot, 1), part],
            zs.at[step - 1], recv, ring(flip[step], x, k),
        )

    def z_copy(j, step):
        return z_part(cols(j), step, zr.at[j, step - 1])

    def z_pass(j):
        return remote(
            vbuf.at[rows(3, 1), cols(j)], vbuf.at[rows(2, 1), cols(j)],
            zs.at[1], zr.at[j, 1], ring(flip[1], x, k),
        )

    def w_part(part, recv):
        return remote(v_hbm.at[:, part], vbuf.at[rows(4, 1), part], ws, recv, x_mate)

    def w_copy(j):
        return w_part(cols(j), wr.at[j])

    def x_part(part, recv):
        return remote(vbuf.at[rows(1, 3), part], vbuf.at[rows(5, 3), part], xs, recv, x_mate)

    def x_copy(j):
        return x_part(cols(j), xr.at[j])

    def k_part(part, recv):
        return remote(
            vbuf.at[rows(0, half_slots), part], vbuf.at[rows(half_slots, half_slots), part],
            ks, recv, k_mate,
        )

    def k_copy(j):
        return k_part(cols(j), kr.at[j])

    orbitals = c_hbm.shape[0]
    cut = orbitals // 32 * 16
    halves = (pl.ds(0, cut), pl.ds(cut, orbitals - cut))

    def c_over(half):
        return remote(
            c_hbm.at[halves[half], :], cbuf.at[g, halves[half], :], cs.at[0], cr.at[0], y_mate
        )

    def c_across(half):
        part = cbuf.at[1 - g, halves[half], :]
        return remote(part, part, cs.at[1], cr.at[1], k_mate)

    def by_core(f):
        for half in range(2):
            pl.when(k == half)(functools.partial(f, half))

    def looped(f, start, stop):
        def body(j, carry):
            f(j)
            return carry

        lax.fori_loop(start, stop, body, 0)

    v_local.start()
    looped(lambda j: d_copy(j).start(), 0, last)
    d_copy(last).start()
    c_local.start()

    barrier = pltpu.get_barrier_semaphore()
    mates = [ring(flip[step], x, k) for step in (1, 2, 3)] + [x_mate, k_mate, y_mate]
    for mate in mates:
        pl.semaphore_signal(barrier, inc=1, device_id=mate, device_id_type=MESH)
    pl.semaphore_wait(barrier, len(mates))

    def own_send(i):
        def send(j):
            z_copy(j, 3).start()
            pl.when(inner == 0)(lambda: z_copy(j, 2).start())
            pl.when((inner == 0) | (i < BEFORE))(lambda: z_copy(j, 1).start())
            w_copy(j).start()

        each(i, send)

    looped(own_send, 0, PACED)
    pl.when(k == 0)(lambda: looped(own_send, PACED, PARTS))
    acc[...] = jnp.zeros_like(acc)
    bcc[...] = jnp.zeros_like(bcc)
    v_local.wait()

    def z_relay(j):
        z_copy(j, 3).wait_recv()
        z_pass(j).start()
        pl.when(j + BEFORE <= last)(
            lambda: each(j + BEFORE, lambda i: z_copy(i, 1).start())
        )

    def x_relay(j):
        z_copy(j, 1).wait_recv()
        z_copy(j, 2).wait_recv()
        pl.when(inner == 0)(lambda: z_copy(j, 3).wait_recv())
        x_copy(j).start()

    def k_relay(j):
        w_copy(j).wait_recv()
        x_copy(j).wait_recv()
        k_copy(j).start()

    def landed(j):
        k_copy(j).wait_recv()
        d_copy(j).wait()

    top = acc.shape[0]

    def add_product(part):
        upper = lax.dot_general(
            dbuf[0:top, part], vbuf[:, part], NT, preferred_element_type=jnp.float32
        )
        lower = lax.dot_general(
            vbuf[:, part], dbuf[top:, part], NT, preferred_element_type=jnp.float32
        )
        acc[...] += upper
        bcc[...] += lower

    def multiply(j):
        each(j, landed)
        add_product(pl.ds(pl.multiple_of(j * unit, LANES), unit))
        if columns > PARTS * unit:
            spare = pl.ds(PARTS * unit, columns - PARTS * unit)
            pl.when(j == PARTS - 1)(lambda: add_product(spare))

        @pl.when(j == 0)
        def _():
            pl.semaphore_signal(other, inc=1, device_id=y_mate, device_id_type=MESH)

    def c_pass(half):
        c_over(half).wait_recv()
        c_across(half).start()

    def step_of(t):
        pl.when(inner == 1)(lambda: each(t, z_relay))
        pl.when((k == 1) & (t + PACED < PARTS))(lambda: own_send(t + PACED))
        middle = t - Z_LAG
        pl.when(middle >= 0)(lambda: each(middle, x_relay))
        before = t - X_LAG
        pl.when(before >= 0)(lambda: each(before, k_relay))
        done = t - K_LAG
        pl.when(done >= 0)(lambda: multiply(done))
        pl.when(t == 1)(lambda: by_core(lambda half: c_over(half).start()))
        pl.when(t == PARTS + 3)(lambda: by_core(c_pass))

    looped(step_of, 0, PARTS + K_LAG)

    gsend[:, 0, 0:top] = acc[...].T
    gsend[:, 0, top:] = bcc[...]
    pl.semaphore_wait(other, 1)

    own_place = grecv.at[g, r % groups, r // groups]

    def g_copy(step):
        target = (linear + step) % total
        tr, tg = device(target)
        return remote(gsend.at[slot_of(tr) * width + tg], own_place, gs, gr, (tr, tg))

    looped(lambda step: g_copy(step).start(), 1, total)
    pltpu.make_async_copy(gsend.at[g], own_place, gr).start()

    for step in (1, 2, 3):
        z_part(whole, step, zr.at[0, step - 1]).wait_send()
    w_part(whole, wr.at[0]).wait_send()
    x_part(whole, xr.at[0]).wait_send()
    k_part(whole, kr.at[0]).wait_send()
    c_local.wait()

    def c_done(half):
        c_over(half).wait_send()
        c_across(half).wait_send()
        c_across(1 - half).wait_recv()

    by_core(c_done)
    pltpu.make_async_copy(grecv, grecv, gr).wait()

    total_out = None
    for half in range(groups):
        gam = sum(grecv[src, half, :, 0, :] for src in range(1, groups)) + grecv[0, half, :, 0, :]
        high = gam.astype(jnp.bfloat16).astype(jnp.float32)
        left = gam - high
        mid = left.astype(jnp.bfloat16).astype(jnp.float32)
        low = left - mid
        stacked = jnp.concatenate([high, mid, low], axis=0).astype(jnp.bfloat16)
        part = lax.dot_general(stacked, cbuf[half], NT, preferred_element_type=jnp.float32)
        total_out = part if total_out is None else total_out + part
    o_ref[...] = total_out[2 * occ:] + total_out[occ:2 * occ] + total_out[:occ]
    outgoing = gsend.at[pl.ds(0, total - 1)]
    pltpu.make_async_copy(outgoing, outgoing, gs).wait()


def fused(slab, groups, density, chol_vectors, virt_coef):
    rows, columns = density.shape
    width = chol_vectors.shape[1]
    coef_rows, orbitals = virt_coef.shape
    total, occ = slab * groups, slab // groups
    top = -(-rows // 256) // 2 * 256
    dma = pltpu.SemaphoreType.DMA
    out = pl.pallas_call(
        functools.partial(kernel, slab, groups),
        out_shape=jax.ShapeDtypeStruct((occ, orbitals), jnp.float32),
        in_specs=[pl.BlockSpec(memory_space=pl.ANY)] * 3,
        out_specs=pl.BlockSpec(memory_space=pltpu.VMEM),
        scratch_shapes=[
            pltpu.VMEM((rows, columns), density.dtype),
            pltpu.VMEM((slab * width, columns), chol_vectors.dtype),
            pltpu.VMEM((groups, orbitals, coef_rows), virt_coef.dtype),
            pltpu.VMEM((top, slab * width), jnp.float32),
            pltpu.VMEM((slab * width, rows - top), jnp.float32),
            pltpu.VMEM((slab * width, 1, rows), jnp.float32),
            pltpu.VMEM((groups, groups, occ, 1, rows), jnp.float32),
            dma((PARTS,)), dma((2,)),
            dma((3,)), dma((PARTS, 3)), dma, dma((PARTS,)),
            dma, dma((PARTS,)), dma, dma((PARTS,)),
            dma((2,)), dma((2,)), dma, dma, pltpu.SemaphoreType.REGULAR,
        ],
        compiler_params=pltpu.CompilerParams(
            collective_id=0, has_side_effects=True, vmem_limit_bytes=VMEM_BYTES
        ),
    )(density, chol_vectors.T, virt_coef.T)
    return out.reshape(occ, 1, orbitals)


def on_device(slab, groups, density, chol_vectors, virt_coef):
    rows, columns = density.shape
    width = chol_vectors.shape[1]
    padded = (columns + LANES) * (rows + 16 + slab * width) * 2
    fits = padded + 8 * virt_coef.size < VMEM_BYTES - (6 << 20)
    paired = groups == 2 and width == groups and slab == 16
    if fits and paired and rows == virt_coef.shape[0] and chunk_of(columns) > 0 and rows > 256:
        return fused(slab, groups, density, chol_vectors, virt_coef)
    return by_collectives(density, chol_vectors, virt_coef)


def solution(mesh):
    in_specs = (P("ia", "jb"), P("jb", "ia"), P("jb", None))
    out_specs = P(None, ("ia", "jb"), None)
    body = functools.partial(on_device, mesh.shape["ia"], mesh.shape["jb"])
    return jax.shard_map(body, mesh=mesh, in_specs=in_specs, out_specs=out_specs, check_vma=False)
```

```python
import functools

import jax
import jax.numpy as jnp
from jax import lax
from jax.experimental import pallas as pl
from jax.experimental.pallas import tpu as pltpu
from jax.sharding import PartitionSpec as P

MESH = pl.DeviceIdType.MESH
LANES = 128
VMEM_BYTES = 67043328
PARTS = 13
BEFORE = 1
PACED = 3
Z_LAG = 1
X_LAG = 4
K_LAG = 5
NT = (((1,), (1,)), ((), ()))


def from_root(value, axis, source):
    kept = jnp.where(lax.axis_index(axis) == source, value, 0).astype(value.dtype)
    return lax.psum(kept, axis)


def by_collectives(density, chol_vectors, virt_coef):
    row_count = density.shape[0]
    groups = lax.axis_size("jb")
    slab_devices = lax.axis_size("ia")
    all_vectors = lax.all_gather(chol_vectors, "ia", axis=1, tiled=True)
    gamma_part = jnp.dot(density, all_vectors, preferred_element_type=jnp.float32)
    owner_row = lax.axis_index("ia") % groups
    coef_block = from_root(virt_coef, "jb", owner_row).astype(jnp.float32)
    chol_count = gamma_part.shape[1]
    group_width = chol_count // slab_devices
    reduced = lax.psum_scatter(
        gamma_part.reshape(row_count, slab_devices, group_width),
        "jb",
        scatter_dimension=2,
        tiled=True,
    )
    summed = jnp.einsum("arq,an->rqn", reduced, coef_block, precision=lax.Precision.HIGHEST)
    regrouped = lax.all_to_all(summed, "ia", split_axis=0, concat_axis=0, tiled=True)
    occ_slab = slab_devices // groups
    return jnp.sum(
        regrouped.reshape(occ_slab, groups, regrouped.shape[1], regrouped.shape[2]), axis=1
    )


def chunk_of(columns):
    return columns // (PARTS * LANES) * LANES


def kernel(
    slab, groups, d_hbm, v_hbm, c_hbm, o_ref,
    dbuf, vbuf, cbuf, acc, bcc, gsend, grecv,
    dsem, lsem, zs, zr, ws, wr, xs, xr, ks, kr, cs, cr, gs, gr, other,
):
    width, columns = v_hbm.shape
    unit = chunk_of(columns)
    last = PARTS - 1
    last_size = columns - last * unit
    total = slab * groups
    occ = slab // groups
    half_slots = slab // 2
    r, g = lax.axis_index("ia"), lax.axis_index("jb")
    z, x, k = r // 4, (r // 2) % 2, r % 2
    inner = ((z + 1) // 2) % 2
    linear = r * groups + g

    def ring(zz, xx, kk):
        return ((zz * 2 + xx) * 2 + kk, g)

    flip = {1: z + 1 - 2 * (z % 2), 2: (z + 2) % 4, 3: 3 - z}
    x_mate = ring(z, 1 - x, k)
    k_mate = ring(z, x, 1 - k)
    y_mate = (r, 1 - g)

    def device(lin):
        return (lin // groups, lin % groups)

    def slot_of(rr):
        zz, xx, kk = rr // 4, (rr // 2) % 2, rr % 2
        other_x, other_k = (xx + x) % 2, (kk + k) % 2
        near = jnp.where((zz // 2) == (z // 2), jnp.where(zz == z, 0, 3 - 2 * inner), 0)
        far = jnp.where((zz // 2) == (z // 2), 0, jnp.where(zz + z == 3, 1 + 2 * inner, 2))
        return (other_k * 2 + other_x) * 4 + near + far

    def cols(j):
        if isinstance(j, int) and j == last:
            return pl.ds(last * unit, last_size)
        return pl.ds(pl.multiple_of(j * unit, LANES), unit)

    def each(j, f):
        pl.when(j < last)(lambda: f(j))
        pl.when(j == last)(lambda: f(last))

    whole = pl.ds(0, columns)

    def rows(start, size):
        if isinstance(start, int):
            return pl.ds(start * width, size * width)
        return pl.ds(pl.multiple_of(start * width, width), size * width)

    def d_copy(j):
        return pltpu.make_async_copy(d_hbm.at[:, cols(j)], dbuf.at[:, cols(j)], dsem.at[j])

    v_local = pltpu.make_async_copy(v_hbm, vbuf.at[rows(0, 1), :], lsem.at[0])
    c_local = pltpu.make_async_copy(c_hbm, cbuf.at[g], lsem.at[1])

    def remote(source, dest, send, recv, target):
        return pltpu.make_async_remote_copy(
            source, dest, send, recv, device_id=target, device_id_type=MESH
        )

    def z_part(part, step, recv):
        slot = 2 if step == 2 else 1 + 2 * inner
        return remote(
            v_hbm.at[:, part], vbuf.at[rows(slot, 1), part],
            zs.at[step - 1], recv, ring(flip[step], x, k),
        )

    def z_copy(j, step):
        return z_part(cols(j), step, zr.at[j, step - 1])

    def z_pass(j):
        return remote(
            vbuf.at[rows(3, 1), cols(j)], vbuf.at[rows(2, 1), cols(j)],
            zs.at[1], zr.at[j, 1], ring(flip[1], x, k),
        )

    def w_part(part, recv):
        return remote(v_hbm.at[:, part], vbuf.at[rows(4, 1), part], ws, recv, x_mate)

    def w_copy(j):
        return w_part(cols(j), wr.at[j])

    def x_part(part, recv):
        return remote(vbuf.at[rows(1, 3), part], vbuf.at[rows(5, 3), part], xs, recv, x_mate)

    def x_copy(j):
        return x_part(cols(j), xr.at[j])

    def k_part(part, recv):
        return remote(
            vbuf.at[rows(0, half_slots), part], vbuf.at[rows(half_slots, half_slots), part],
            ks, recv, k_mate,
        )

    def k_copy(j):
        return k_part(cols(j), kr.at[j])

    orbitals = c_hbm.shape[0]
    cut = orbitals // 32 * 16
    halves = (pl.ds(0, cut), pl.ds(cut, orbitals - cut))

    def c_over(half):
        return remote(
            c_hbm.at[halves[half], :], cbuf.at[g, halves[half], :], cs.at[0], cr.at[0], y_mate
        )

    def c_across(half):
        part = cbuf.at[1 - g, halves[half], :]
        return remote(part, part, cs.at[1], cr.at[1], k_mate)

    def by_core(f):
        for half in range(2):
            pl.when(k == half)(functools.partial(f, half))

    def looped(f, start, stop):
        def body(j, carry):
            f(j)
            return carry

        lax.fori_loop(start, stop, body, 0)

    v_local.start()
    looped(lambda j: d_copy(j).start(), 0, last)
    d_copy(last).start()
    c_local.start()

    barrier = pltpu.get_barrier_semaphore()
    mates = [ring(flip[step], x, k) for step in (1, 2, 3)] + [x_mate, k_mate, y_mate]
    for mate in mates:
        pl.semaphore_signal(barrier, inc=1, device_id=mate, device_id_type=MESH)
    pl.semaphore_wait(barrier, len(mates))

    def own_send(i):
        def send(j):
            z_copy(j, 3).start()
            pl.when(inner == 0)(lambda: z_copy(j, 2).start())
            pl.when((inner == 0) | (i < BEFORE))(lambda: z_copy(j, 1).start())
            w_copy(j).start()

        each(i, send)

    looped(own_send, 0, PACED)
    pl.when(k == 0)(lambda: looped(own_send, PACED, PARTS))
    acc[...] = jnp.zeros_like(acc)
    bcc[...] = jnp.zeros_like(bcc)
    v_local.wait()

    def z_relay(j):
        z_copy(j, 3).wait_recv()
        z_pass(j).start()
        pl.when(j + BEFORE <= last)(
            lambda: each(j + BEFORE, lambda i: z_copy(i, 1).start())
        )

    def x_relay(j):
        z_copy(j, 1).wait_recv()
        z_copy(j, 2).wait_recv()
        pl.when(inner == 0)(lambda: z_copy(j, 3).wait_recv())
        x_copy(j).start()

    def k_relay(j):
        w_copy(j).wait_recv()
        x_copy(j).wait_recv()
        k_copy(j).start()

    def landed(j):
        k_copy(j).wait_recv()
        d_copy(j).wait()

    top = acc.shape[0]

    def add_product(part):
        upper = lax.dot_general(
            dbuf[0:top, part], vbuf[:, part], NT, preferred_element_type=jnp.float32
        )
        lower = lax.dot_general(
            vbuf[:, part], dbuf[top:, part], NT, preferred_element_type=jnp.float32
        )
        acc[...] += upper
        bcc[...] += lower

    def multiply(j):
        each(j, landed)
        add_product(pl.ds(pl.multiple_of(j * unit, LANES), unit))
        if columns > PARTS * unit:
            spare = pl.ds(PARTS * unit, columns - PARTS * unit)
            pl.when(j == PARTS - 1)(lambda: add_product(spare))

        @pl.when(j == 0)
        def _():
            pl.semaphore_signal(other, inc=1, device_id=y_mate, device_id_type=MESH)

    def c_pass(half):
        c_over(half).wait_recv()
        c_across(half).start()

    def step_of(t):
        pl.when(inner == 1)(lambda: each(t, z_relay))
        pl.when((k == 1) & (t + PACED < PARTS))(lambda: own_send(t + PACED))
        middle = t - Z_LAG
        pl.when(middle >= 0)(lambda: each(middle, x_relay))
        before = t - X_LAG
        pl.when(before >= 0)(lambda: each(before, k_relay))
        done = t - K_LAG
        pl.when(done >= 0)(lambda: multiply(done))
        pl.when(t == 1)(lambda: by_core(lambda half: c_over(half).start()))
        pl.when(t == PARTS + 3)(lambda: by_core(c_pass))

    looped(step_of, 0, PARTS + K_LAG)

    gsend[:, 0, 0:top] = acc[...].T
    gsend[:, 0, top:] = bcc[...]
    pl.semaphore_wait(other, 1)

    own_place = grecv.at[g, r % groups, r // groups]

    def g_copy(step):
        target = (linear + step) % total
        tr, tg = device(target)
        return remote(gsend.at[slot_of(tr) * width + tg], own_place, gs, gr, (tr, tg))

    looped(lambda step: g_copy(step).start(), 1, total)
    pltpu.make_async_copy(gsend.at[g], own_place, gr).start()

    for step in (1, 2, 3):
        z_part(whole, step, zr.at[0, step - 1]).wait_send()
    w_part(whole, wr.at[0]).wait_send()
    x_part(whole, xr.at[0]).wait_send()
    k_part(whole, kr.at[0]).wait_send()
    c_local.wait()

    def c_done(half):
        c_over(half).wait_send()
        c_across(half).wait_send()
        c_across(1 - half).wait_recv()

    by_core(c_done)
    pltpu.make_async_copy(grecv, grecv, gr).wait()

    total_out = None
    for half in range(groups):
        gam = sum(grecv[src, half, :, 0, :] for src in range(1, groups)) + grecv[0, half, :, 0, :]
        high = gam.astype(jnp.bfloat16).astype(jnp.float32)
        left = gam - high
        mid = left.astype(jnp.bfloat16).astype(jnp.float32)
        low = left - mid
        stacked = jnp.concatenate([high, mid, low], axis=0).astype(jnp.bfloat16)
        part = lax.dot_general(stacked, cbuf[half], NT, preferred_element_type=jnp.float32)
        total_out = part if total_out is None else total_out + part
    o_ref[...] = total_out[2 * occ:] + total_out[occ:2 * occ] + total_out[:occ]
    outgoing = gsend.at[pl.ds(0, total - 1)]
    pltpu.make_async_copy(outgoing, outgoing, gs).wait()


def fused(slab, groups, density, chol_vectors, virt_coef):
    rows, columns = density.shape
    width = chol_vectors.shape[1]
    coef_rows, orbitals = virt_coef.shape
    total, occ = slab * groups, slab // groups
    top = -(-rows // 256) // 2 * 256
    dma = pltpu.SemaphoreType.DMA
    out = pl.pallas_call(
        functools.partial(kernel, slab, groups),
        out_shape=jax.ShapeDtypeStruct((occ, orbitals), jnp.float32),
        in_specs=[pl.BlockSpec(memory_space=pl.ANY)] * 3,
        out_specs=pl.BlockSpec(memory_space=pltpu.VMEM),
        scratch_shapes=[
            pltpu.VMEM((rows, columns), density.dtype),
            pltpu.VMEM((slab * width, columns), chol_vectors.dtype),
            pltpu.VMEM((groups, orbitals, coef_rows), virt_coef.dtype),
            pltpu.VMEM((top, slab * width), jnp.float32),
            pltpu.VMEM((slab * width, rows - top), jnp.float32),
            pltpu.VMEM((slab * width, 1, rows), jnp.float32),
            pltpu.VMEM((groups, groups, occ, 1, rows), jnp.float32),
            dma((PARTS,)), dma((2,)),
            dma((3,)), dma((PARTS, 3)), dma, dma((PARTS,)),
            dma, dma((PARTS,)), dma, dma((PARTS,)),
            dma((2,)), dma((2,)), dma, dma, pltpu.SemaphoreType.REGULAR,
        ],
        compiler_params=pltpu.CompilerParams(
            collective_id=0, has_side_effects=True, vmem_limit_bytes=VMEM_BYTES
        ),
    )(density, chol_vectors.T, virt_coef.T)
    return out.reshape(occ, 1, orbitals)


def on_device(slab, groups, density, chol_vectors, virt_coef):
    rows, columns = density.shape
    width = chol_vectors.shape[1]
    padded = (columns + LANES) * (rows + 16 + slab * width) * 2
    fits = padded + 8 * virt_coef.size < VMEM_BYTES - (6 << 20)
    paired = groups == 2 and width == groups and slab == 16
    if fits and paired and rows == virt_coef.shape[0] and chunk_of(columns) > 0 and rows > 256:
        return fused(slab, groups, density, chol_vectors, virt_coef)
    return by_collectives(density, chol_vectors, virt_coef)


def solution(mesh):
    in_specs = (P("ia", "jb"), P("jb", "ia"), P("jb", None))
    out_specs = P(None, ("ia", "jb"), None)
    body = functools.partial(on_device, mesh.shape["ia"], mesh.shape["jb"])
    return jax.shard_map(body, mesh=mesh, in_specs=in_specs, out_specs=out_specs, check_vma=False)
```
